32 devices in a mesh: dp: 2 (over y), tm: 8 (over z, core), height: 2 (over x).
Axes of the slice: x: 2, y: 2, z: 4, core: 2. Of those that a mesh axis runs over, the one named last changes fastest.
Arguments:
- clip_input: bfloat16 [2, 32, 8, 96, 128], P('dp', 'tm', 'height'), may hold values from -6 to 6
- cotangent: bfloat16 [2, 32, 8, 96, 128], P('dp', 'tm', 'height'), may hold values from -6 to 6
- first_kernel: bfloat16 [2592, 96], replicated, may hold values from -0.125 to 0.125
- second_kernel: bfloat16 [2592, 96], replicated, may hold values from -0.125 to 0.125
Outputs:
- block_output: float32 [2, 32, 8, 96, 128], P('dp', 'tm', 'height')
- input_grad: float32 [2, 32, 8, 96, 128], P('dp', 'tm', 'height')
- first_grad: float32 [2592, 96], P('dp')
- second_grad: float32 [2592, 96], P('dp')
The draws below stay inside these ranges and needn't reach their ends.
All inputs are finite; a program needn't handle non-finite values.
Results may differ from the reference program's by a relative error of at most 0.0048.
Values may be sent and summed in bfloat16 or wider, within the bound.
A program may use at most 64 MiB of HBM per device.

```python
import math
import jax
import jax.numpy as jnp
from jax import lax

C = 96
COLS = 128
CLIPS = 2
FRAMES = 32
ROWS = 8


def shard_levels(rng, shape, pieces, least, largest):
    loudness, own = 1.0, jax.random.fold_in(rng, 6)
    for dim, blocks in pieces:
        heights = jnp.exp(jax.random.uniform(jax.random.fold_in(own, dim), (blocks,), jnp.float32, least / len(pieces), largest / len(pieces)))
        loudness = loudness * jnp.repeat(heights, shape[dim] // blocks).reshape([-1 if axis == dim else 1 for axis in range(len(shape))])
    return loudness


def normal_values(stream_key, shape, width, reach, split=(), kind=jnp.bfloat16):
    values = jax.random.normal(stream_key, shape, jnp.float32) * width
    if len(split) > 0:
        values = shard_levels(stream_key, shape, split, -0.22, 0.18) * values
    return jnp.clip(values, min=-reach, max=reach).astype(kind)


def setup_inputs(seed: int = 0) -> dict:
    seeds = jax.random.split(jax.random.key(seed), 5)
    clip_input = normal_values(seeds[0], (CLIPS, FRAMES, ROWS, C, COLS), 1.0, 6.0, ((0, 2), (1, 8), (2, 2)))
    cotangent = normal_values(seeds[1], (CLIPS, FRAMES, ROWS, C, COLS), 1.0, 6.0, ((0, 2), (1, 8), (2, 2)))
    first_kernel = normal_values(seeds[2], (27 * C, C), (27 * C) ** -0.5, 0.125)
    second_kernel = normal_values(seeds[3], (27 * C, C), (27 * C) ** -0.5, 0.125)
    return dict(clip_input=clip_input, cotangent=cotangent, first_kernel=first_kernel, second_kernel=second_kernel)


EPSILON = 1e-06

def norm_silu(field):
    factor = lax.rsqrt(lax.optimization_barrier(jnp.mean(field * field, axis=2, keepdims=True)) + EPSILON)
    return jax.nn.silu(field * factor)

def conv_clip(field, kernel):
    channels = field.shape[2]
    left_side = jnp.transpose(field, (2, 0, 1, 3))[None]
    right_side = jnp.transpose(kernel.reshape(3, 3, 3, channels, channels), (4, 3, 0, 1, 2))
    result = lax.conv_general_dilated(left_side, right_side, (1, 1, 1), ((2, 0), (1, 1), (1, 1)), precision=lax.Precision.HIGHEST)
    return jnp.transpose(result[0], (1, 2, 0, 3))

def to_bf16_and_back(value):
    return lax.optimization_barrier(value.astype(jnp.bfloat16)).astype(jnp.float32)

def reference(clip_input, cotangent, first_kernel, second_kernel):
    kernel_one = first_kernel.astype(jnp.float32)
    kernel_two = second_kernel.astype(jnp.float32)

    def one_clip(paired):
        source = paired[0].astype(jnp.float32)
        upstream = paired[1].astype(jnp.float32)
        first_act = to_bf16_and_back(norm_silu(source))
        middle = conv_clip(first_act, kernel_one)
        second_act = to_bf16_and_back(norm_silu(middle))
        branch = conv_clip(second_act, kernel_two)
        block_output = source + branch
        unused, pull_two = jax.vjp(conv_clip, second_act, kernel_two)
        second_back, second_term = pull_two(upstream)
        unused, pull_mid = jax.vjp(norm_silu, middle)
        middle_grad = to_bf16_and_back(pull_mid(second_back)[0])
        unused, pull_one = jax.vjp(conv_clip, first_act, kernel_one)
        first_back, first_term = pull_one(middle_grad)
        unused, pull_src = jax.vjp(norm_silu, source)
        input_grad = upstream + pull_src(first_back)[0]
        return (block_output, input_grad, first_term, second_term)
    outputs, grads_in, first_terms, second_terms = lax.map(one_clip, (clip_input, cotangent))
    factor = 1.0 / math.sqrt(CLIPS * FRAMES * ROWS * COLS)
    first_grad = lax.optimization_barrier(jnp.sum(first_terms, axis=0)) * factor
    second_grad = lax.optimization_barrier(jnp.sum(second_terms, axis=0)) * factor
    return (outputs, grads_in, first_grad, second_grad)
```

```python
import functools
import math

import jax
import jax.numpy as jnp
from jax import lax
from jax.experimental import pallas as pl
from jax.experimental.pallas import tpu as pltpu
from jax.sharding import PartitionSpec as P

EPSILON = 1e-06


def extended_2(array, sides, width):
    for axis, dim in sides:
        peers, length = (lax.axis_size(axis), array.shape[dim])
        up = [(i, (i + 1) % peers) for i in range(peers - 1)]
        down = [(j, i) for i, j in up]
        last = lax.slice_in_dim(array, length - width, length, axis=dim)
        first = lax.slice_in_dim(array, 0, width, axis=dim)
        before = lax.ppermute(last, axis, up)
        after = lax.ppermute(first, axis, down)
        array = jnp.concatenate([before, array, after], axis=dim)
    return array


def passed_along(array, axis, by):
    peers = lax.axis_size(axis)
    pairs = [(i, i + by) for i in range(peers) if 0 <= i + by < peers]
    return lax.ppermute(array, axis, pairs)


def norm_silu(field):
    factor = lax.rsqrt(jnp.mean(field * field, axis=2, keepdims=True) + EPSILON)
    return jax.nn.silu(field * factor)


def pad_rows(extended):
    rimmed = extended_2(extended, (("height", 1),), 1)
    return jnp.pad(rimmed, ((0, 0), (0, 0), (0, 0), (1, 1)))


def time_stack(padded, tap_row, tap_col, frames):
    row_count = padded.shape[1] - 2
    col_count = padded.shape[3] - 2
    window = padded[:, tap_row : tap_row + row_count, :, tap_col : tap_col + col_count]
    return jnp.concatenate([window[offset : offset + frames] for offset in range(3)], axis=2)


def local_conv(padded, kernel, frames):
    channels = padded.shape[2]
    summed = None
    for tap_row in range(3):
        for tap_col in range(3):
            stacked = time_stack(padded, tap_row, tap_col, frames)
            weight = kernel[:, tap_row, tap_col].reshape(3 * channels, kernel.shape[4])
            partial_sum = jnp.einsum(
                "frkw,kd->frdw", stacked, weight, preferred_element_type=jnp.float32
            )
            summed = partial_sum if summed is None else summed + partial_sum
    return summed


def kernel_grad(padded, grad_out, frames):
    channels = padded.shape[2]
    row_list = []
    for tap_row in range(3):
        col_list = []
        for tap_col in range(3):
            stacked = time_stack(padded, tap_row, tap_col, frames)
            piece = jnp.einsum(
                "frkw,frdw->kd", stacked, grad_out, preferred_element_type=jnp.float32
            )
            col_list.append(piece.reshape(3, channels, grad_out.shape[2]))
        row_list.append(jnp.stack(col_list, axis=1))
    gathered = jnp.stack(row_list, axis=1)
    return gathered.reshape(27 * channels, grad_out.shape[2])


def flipped(kernel):
    return jnp.swapaxes(kernel[::-1, ::-1, ::-1], 3, 4)


def reduce_body(sizes, parts, total, first, wide, narrow_dp, got_dp, narrow_h, got_h, wide_z, got_z, mine, send, recv):
    dp, heights, depth = sizes
    tm_index = lax.axis_index("tm")
    core, level = tm_index % 2, tm_index // 2
    clip, half = lax.axis_index("dp"), lax.axis_index("height")
    barrier = pltpu.get_barrier_semaphore()
    partner = {"tm": level * 2 + 1 - core}
    clip_peers = [(clip + step) % dp for step in range(1, dp)]
    half_peers = [(half + step) % heights for step in range(1, heights)]
    level_peers = [(level + step) % depth for step in range(1, depth)]
    places = [partner]
    places += [{"dp": peer} for peer in clip_peers]
    places += [{"height": peer} for peer in half_peers]
    places += [{"tm": peer * 2 + core} for peer in level_peers]
    for place in places:
        pl.semaphore_signal(barrier, inc=1, device_id=place, device_id_type=pl.DeviceIdType.MESH)
    pl.semaphore_wait(barrier, len(places))
    used = [0]

    def send_to(source, target, place):
        slot = used[0]
        used[0] += 1
        copy = pltpu.make_async_remote_copy(
            src_ref=source,
            dst_ref=target,
            send_sem=send.at[slot],
            recv_sem=recv.at[slot],
            device_id=place,
            device_id_type=pl.DeviceIdType.MESH,
        )
        copy.start()
        return copy

    copy = send_to(parts.at[1 - core], first, partner)
    copy.wait()
    for index in range(dp):
        summed = parts[core, index] + first[index]
        wide[index] = summed
        narrow_dp[index] = summed.astype(jnp.bfloat16)
    copies = [
        send_to(narrow_dp.at[peer], got_dp.at[step], {"dp": peer})
        for step, peer in enumerate(clip_peers)
    ]
    for copy in copies:
        copy.wait()
    summed = wide[clip]
    for step in range(dp - 1):
        summed = summed + got_dp[step].astype(jnp.float32)
    wide[0] = summed
    narrow_h[...] = summed.astype(jnp.bfloat16)
    copies = [
        send_to(narrow_h.at[peer], got_h.at[step], {"height": peer})
        for step, peer in enumerate(half_peers)
    ]
    for copy in copies:
        copy.wait()
    summed = wide[0, half]
    for step in range(heights - 1):
        summed = summed + got_h[step].astype(jnp.float32)
    wide_z[...] = summed
    copies = [
        send_to(wide_z.at[peer], got_z.at[step], {"tm": peer * 2 + core})
        for step, peer in enumerate(level_peers)
    ]
    for copy in copies:
        copy.wait()
    summed = wide_z[level]
    for step in range(depth - 1):
        summed = summed + got_z[step]
    mine[core, half, level] = summed.astype(jnp.bfloat16)
    own = mine.at[core, half, level]
    copies = [send_to(own, own, {"tm": peer * 2 + core}) for peer in level_peers]
    for copy in copies:
        copy.wait()
    own = mine.at[core, half]
    copies = [send_to(own, own, {"height": peer}) for peer in half_peers]
    for copy in copies:
        copy.wait()
    own = mine.at[core]
    copy = send_to(own, own, partner)
    copy.wait()
    total[...] = mine[...].astype(jnp.float32)


def packed(piece):
    quarter = piece.shape[0] // 4
    width = piece.shape[1] // 3
    rest = piece[3 * quarter :]
    side = jnp.concatenate([rest[:, i * width : (i + 1) * width] for i in range(3)], axis=0)
    return jnp.concatenate([piece[: 3 * quarter], side], axis=1)


def unpacked(block, channels):
    quarter = block.shape[0] // 3
    side = block[:, channels:]
    rest = jnp.concatenate([side[i * quarter : (i + 1) * quarter] for i in range(3)], axis=1)
    return jnp.concatenate([block[:, :channels], rest], axis=0)


def reduced(terms):
    dp, heights, depth = (lax.axis_size("dp"), lax.axis_size("height"), lax.axis_size("tm") // 2)
    channels = terms[0].shape[1]
    rows = terms[0].shape[0] // dp
    chunks = []
    for index in range(dp):
        chunks.append(
            jnp.concatenate([packed(term[index * rows : (index + 1) * rows]) for term in terms], axis=0)
        )
    pieces = 2 * heights * depth
    length = chunks[0].shape[0]
    lanes = chunks[0].shape[1]
    block = -(-length // (pieces * 16)) * 16
    stacked = jnp.stack([jnp.pad(chunk, ((0, pieces * block - length), (0, 0))) for chunk in chunks])
    stacked = stacked.reshape(dp, 2, heights, depth, block, lanes).swapaxes(0, 1)
    tail = (block, lanes)
    copies = 2 + (dp - 1) + 2 * (heights - 1) + 2 * (depth - 1)
    total = pl.pallas_call(
        functools.partial(reduce_body, (dp, heights, depth)),
        out_shape=jax.ShapeDtypeStruct((2, heights, depth) + tail, jnp.float32),
        in_specs=[pl.BlockSpec(memory_space=pltpu.VMEM)],
        out_specs=pl.BlockSpec(memory_space=pltpu.VMEM),
        scratch_shapes=[
            pltpu.VMEM((dp, heights, depth) + tail, jnp.float32),
            pltpu.VMEM((dp, heights, depth) + tail, jnp.float32),
            pltpu.VMEM((dp, heights, depth) + tail, jnp.bfloat16),
            pltpu.VMEM((dp - 1, heights, depth) + tail, jnp.bfloat16),
            pltpu.VMEM((heights, depth) + tail, jnp.bfloat16),
            pltpu.VMEM((heights - 1, depth) + tail, jnp.bfloat16),
            pltpu.VMEM((depth,) + tail, jnp.float32),
            pltpu.VMEM((depth - 1,) + tail, jnp.float32),
            pltpu.VMEM((2, heights, depth) + tail, jnp.bfloat16),
            pltpu.SemaphoreType.DMA((copies,)),
            pltpu.SemaphoreType.DMA((copies,)),
        ],
        compiler_params=pltpu.CompilerParams(collective_id=0, has_side_effects=True),
        name="reduce_grads",
    )(stacked)
    flat = total.reshape(pieces * block, lanes)
    each = length // len(terms)
    return [unpacked(flat[i * each : (i + 1) * each], channels) for i in range(len(terms))]


def local(clip_input, cotangent, first_kernel, second_kernel):
    frames = clip_input.shape[1]
    channels = clip_input.shape[3]
    source = clip_input[0]
    upstream = cotangent[0]
    kernel_one = first_kernel.reshape(3, 3, 3, channels, channels)
    kernel_two = second_kernel.reshape(3, 3, 3, channels, channels)

    def extend_back(block):
        earlier = passed_along(block[frames - 2 :], "tm", 1)
        return pad_rows(jnp.concatenate([earlier, block], axis=0))

    def extend_ahead(block):
        later = passed_along(block[:2], "tm", -1)
        return pad_rows(jnp.concatenate([block, later], axis=0))

    source_float = source.astype(jnp.float32)
    first_act = norm_silu(source_float).astype(jnp.bfloat16)
    first_padded = extend_back(first_act)
    middle = local_conv(first_padded, kernel_one, frames)
    second_act = norm_silu(middle).astype(jnp.bfloat16)
    second_padded = extend_back(second_act)
    branch = local_conv(second_padded, kernel_two, frames)
    block_output = source_float + branch
    second_back = local_conv(extend_ahead(upstream), flipped(kernel_two), frames)
    unused, pull_mid = jax.vjp(norm_silu, middle)
    middle_grad = pull_mid(second_back)[0].astype(jnp.bfloat16)
    first_back = local_conv(extend_ahead(middle_grad), flipped(kernel_one), frames)
    unused, pull_src = jax.vjp(norm_silu, source_float)
    input_grad = upstream.astype(jnp.float32) + pull_src(first_back)[0]
    positions = (
        frames
        * source.shape[1]
        * source.shape[3]
        * lax.axis_size("dp")
        * lax.axis_size("tm")
        * lax.axis_size("height")
    )
    factor = 1.0 / math.sqrt(positions)
    first_term = kernel_grad(first_padded, middle_grad, frames)
    second_term = kernel_grad(second_padded, upstream, frames)
    first_grad, second_grad = [whole * factor for whole in reduced((first_term, second_term))]
    return (block_output[None], input_grad[None], first_grad, second_grad)


def solution(mesh):
    return jax.shard_map(
        local,
        mesh=mesh,
        in_specs=(
            P("dp", "tm", "height", None, None),
            P("dp", "tm", "height", None, None),
            P(),
            P(),
        ),
        out_specs=(
            P("dp", "tm", "height", None, None),
            P("dp", "tm", "height", None, None),
            P("dp", None),
            P("dp", None),
        ),
        check_vma=False,
    )
```

```python
import functools
import math

import jax
import jax.numpy as jnp
from jax import lax
from jax.experimental import pallas as pl
from jax.experimental.pallas import tpu as pltpu
from jax.sharding import PartitionSpec as P

EPSILON = 1e-06
MESH_IDS = pl.DeviceIdType.MESH


def factor_of(value):
    return lax.rsqrt(jnp.mean(value * value, axis=0, keepdims=True) + EPSILON)


def act(value):
    scaled = value * factor_of(value)
    return scaled / (1.0 + jnp.exp(-scaled))


def act_back(value, grad):
    factor = factor_of(value)
    scaled = value * factor
    gate = 1.0 / (1.0 + jnp.exp(-scaled))
    inner = grad * (gate * (1.0 + scaled * (1.0 - gate)))
    return factor * (inner - scaled * jnp.mean(inner * scaled, axis=0, keepdims=True))


def body(
    sizes,
    x,
    cot,
    kernel_one,
    kernel_two,
    flip_one,
    flip_two,
    block_out,
    input_out,
    total,
    acts_one,
    acts_two,
    grads_two,
    grads_one,
    middle,
    second_act,
    middle_grad,
    time_halo,
    row_halo,
    corner_halo,
    terms,
    first,
    wide,
    narrow_dp,
    got_dp,
    narrow_h,
    got_h,
    wide_z,
    got_z,
    mine,
    halo_send,
    halo_recv,
    send,
    recv,
):
    dp, heights, depth = sizes
    frames, rows, channels, cols = x.shape
    shards = 2 * depth
    chunk = terms.shape[1] // dp
    shard = lax.axis_index("tm")
    core, level = shard % 2, shard // 2
    clip, half = lax.axis_index("dp"), lax.axis_index("height")
    other = 1 - half
    has_before, has_after = shard > 0, shard < shards - 1
    edge_row = (rows - 1) * other
    halo_row = (rows + 1) * other
    rim_row = (rows + 1) * half

    barrier = pltpu.get_barrier_semaphore()
    partner = {"tm": level * 2 + 1 - core}
    clip_peers = [(clip + step) % dp for step in range(1, dp)]
    level_peers = [(level + step) % depth for step in range(1, depth)]
    places = [partner, {"height": other}]
    places += [{"dp": peer} for peer in clip_peers]
    places += [{"tm": peer * 2 + core} for peer in level_peers]

    def greet(place):
        pl.semaphore_signal(barrier, inc=1, device_id=place, device_id_type=MESH_IDS)

    for place in places:
        greet(place)

    outer = shard + 2 * core - 1
    has_outer = jnp.logical_and(outer >= 0, outer < shards)

    @pl.when(has_outer)
    def _():
        greet({"tm": outer})

    @pl.when(has_before)
    def _():
        greet({"tm": shard - 1, "height": other})

    @pl.when(has_after)
    def _():
        greet({"tm": shard + 1, "height": other})

    near = has_outer.astype(jnp.int32) + has_before.astype(jnp.int32) + has_after.astype(jnp.int32)
    pl.semaphore_wait(barrier, len(places) + near)

    def remote(source, target, sender, receiver, place):
        return pltpu.make_async_remote_copy(
            src_ref=source,
            dst_ref=target,
            send_sem=sender,
            recv_sem=receiver,
            device_id=place,
            device_id_type=MESH_IDS,
        )

    def exchange(own, slot, ahead):
        step = -1 if ahead else 1
        start = 0 if ahead else frames - 2
        goes, comes = (has_before, has_after) if ahead else (has_after, has_before)
        span = pl.ds(start, 2)
        along = remote(own.at[span], time_halo.at[slot], halo_send.at[slot, 0], halo_recv.at[slot, 0], {"tm": shard + step})
        across = remote(own.at[:, edge_row], row_halo.at[slot], halo_send.at[slot, 1], halo_recv.at[slot, 1], {"height": other})
        corner = remote(
            own.at[span, edge_row],
            corner_halo.at[slot],
            halo_send.at[slot, 2],
            halo_recv.at[slot, 2],
            {"tm": shard + step, "height": other},
        )
        across.start()

        @pl.when(goes)
        def _():
            along.start()
            corner.start()

        def arrive():
            across.wait()

            @pl.when(goes)
            def _():
                along.wait_send()
                corner.wait_send()

            @pl.when(comes)
            def _():
                along.wait_recv()
                corner.wait_recv()

        return arrive

    lane = lax.broadcasted_iota(jnp.int32, (channels, cols), 1)

    def place_tile(field, frame, row, value):
        wide_value = value.astype(jnp.float32)
        left = jnp.where(lane == 0, 0.0, pltpu.roll(wide_value, 1, axis=1))
        right = jnp.where(lane == cols - 1, 0.0, pltpu.roll(wide_value, cols - 1, axis=1))
        field[frame, row, 0:channels] = left.astype(jnp.bfloat16)
        field[frame, row, channels : 2 * channels] = value
        field[frame, row, 2 * channels : 3 * channels] = right.astype(jnp.bfloat16)

    def fill_halo(field, slot, ahead, make):
        inside, outside = (0, frames) if ahead else (2, 0)
        comes = has_after if ahead else has_before
        blank = jnp.zeros((3 * channels, cols), jnp.bfloat16)
        for frame in range(frames + 2):
            field[frame, rim_row] = blank

        def row_step(frame, carry):
            place_tile(field, inside + frame, halo_row, make(row_halo[slot, frame]))
            return carry

        lax.fori_loop(0, frames, row_step, 0)

        @pl.when(comes)
        def _():
            def time_step(index, carry):
                frame, row = index // rows, index % rows
                place_tile(field, outside + frame, row + 1, make(time_halo[slot, frame, row]))
                return carry

            lax.fori_loop(0, 2 * rows, time_step, 0)
            for frame in range(2):
                place_tile(field, outside + frame, halo_row, make(corner_halo[slot, frame]))

        @pl.when(jnp.logical_not(comes))
        def _():
            for frame in range(2):
                for row in range(rows + 2):
                    field[outside + frame, row] = blank

    def conv(field, kernel, finish):
        def step(index, carry):
            frame, row = 2 * (index // rows), index % rows
            summed = None
            for tap in range(3):
                pair = [
                    field[frame + tap + side, pl.ds(row, 3)].reshape(9 * channels, cols) for side in range(2)
                ]
                part = jnp.dot(kernel[tap], jnp.concatenate(pair, axis=1), preferred_element_type=jnp.float32)
                summed = part if summed is None else summed + part
            for side in range(2):
                finish(frame + side, row, summed[:, side * cols : (side + 1) * cols])
            return carry

        lax.fori_loop(0, frames // 2 * rows, step, 0)

    def kernel_grad(slot, field, grad):
        def step(index, carry):
            tap, tap_row = index // 3, index % 3
            tiles = [(frame, row) for frame in range(frames) for row in range(rows)]
            left = jnp.concatenate([field[frame + tap, row + tap_row] for frame, row in tiles], axis=1)
            right = jnp.concatenate([grad[frame, row] for frame, row in tiles], axis=1)
            piece = lax.dot_general(left, right, (((1,), (1,)), ((), ())), preferred_element_type=jnp.float32)
            terms[slot, pl.ds(pl.multiple_of(index * 3 * channels, 3 * channels), 3 * channels)] = piece
            return carry

        lax.fori_loop(0, 9, step, 0)

    def as_act(value):
        return act(value.astype(jnp.float32)).astype(jnp.bfloat16)

    x_arrives = exchange(x, 0, False)
    cot_arrives = exchange(cot, 1, True)

    def first_step(index, carry):
        frame, row = index // rows, index % rows
        place_tile(acts_one, frame + 2, row + 1, as_act(x[frame, row]))
        place_tile(grads_two, frame, row + 1, cot[frame, row])
        return carry

    lax.fori_loop(0, frames * rows, first_step, 0)
    x_arrives()
    fill_halo(acts_one, 0, False, as_act)

    def finish_middle(frame, row, value):
        middle[frame, row] = value
        rounded = act(value).astype(jnp.bfloat16)
        second_act[frame, row] = rounded
        place_tile(acts_two, frame + 2, row + 1, rounded)

    conv(acts_one, kernel_one, finish_middle)
    act_arrives = exchange(second_act, 2, False)
    cot_arrives()
    fill_halo(grads_two, 1, True, lambda value: value)

    def finish_back(frame, row, value):
        rounded = act_back(middle[frame, row], value).astype(jnp.bfloat16)
        middle_grad[frame, row] = rounded
        place_tile(grads_one, frame, row + 1, rounded)

    conv(grads_two, flip_two, finish_back)
    grad_arrives = exchange(middle_grad, 3, True)

    used = [0]

    def send_to(source, target, place):
        slot = used[0]
        used[0] += 1
        copy = remote(source, target, send.at[slot], recv.at[slot], place)
        copy.start()
        return copy

    kernel_grad(0, acts_one, middle_grad)
    act_arrives()
    fill_halo(acts_two, 2, False, lambda value: value)
    kernel_grad(1, acts_two, cot)
    swap = send_to(terms.at[1 - core], first, partner)

    def finish_branch(frame, row, value):
        block_out[frame, row] = x[frame, row].astype(jnp.float32) + value

    def finish_input(frame, row, value):
        back = act_back(x[frame, row].astype(jnp.float32), value)
        input_out[frame, row] = cot[frame, row].astype(jnp.float32) + back

    conv(acts_two, kernel_two, finish_branch)
    swap.wait()
    padded = wide.shape[1]
    for index in range(dp):
        span = pl.ds(index * chunk, chunk)
        summed = terms[core, span] + first[span]
        if padded > chunk:
            summed = jnp.concatenate([summed, jnp.zeros((padded - chunk, channels), jnp.float32)], axis=0)
        wide[index] = summed
        narrow_dp[index] = summed.astype(jnp.bfloat16)
    copies = [send_to(narrow_dp.at[peer], got_dp.at[i], {"dp": peer}) for i, peer in enumerate(clip_peers)]
    grad_arrives()
    fill_halo(grads_one, 3, True, lambda value: value)
    conv(grads_one, flip_one, finish_input)
    for copy in copies:
        copy.wait()
    summed = wide[clip]
    for i in range(dp - 1):
        summed = summed + got_dp[i].astype(jnp.float32)
    wide[0] = summed
    narrow_h[...] = summed.astype(jnp.bfloat16).reshape(narrow_h.shape)
    send_to(narrow_h.at[other], got_h, {"height": other}).wait()
    block = wide_z.shape[1]
    mine_rows = pl.ds(pl.multiple_of(half * (depth * block), depth * block), depth * block)
    summed = wide[0, mine_rows] + got_h[...].astype(jnp.float32)
    wide_z[...] = summed.reshape(wide_z.shape)
    copies = [
        send_to(wide_z.at[peer], got_z.at[i], {"tm": peer * 2 + core}) for i, peer in enumerate(level_peers)
    ]
    for copy in copies:
        copy.wait()
    summed = wide_z[level]
    for i in range(depth - 1):
        summed = summed + got_z[i]
    mine[core, half, level] = summed.astype(jnp.bfloat16)
    own = mine.at[core, half, level]
    copies = [send_to(own, own, {"tm": peer * 2 + core}) for peer in level_peers]
    for copy in copies:
        copy.wait()
    own = mine.at[core, half]
    send_to(own, own, {"height": other}).wait()
    own = mine.at[core]
    send_to(own, own, partner).wait()
    total[...] = mine[...].astype(jnp.float32)


def local(clip_input, cotangent, first_kernel, second_kernel):
    dp, heights, depth = (lax.axis_size("dp"), lax.axis_size("height"), lax.axis_size("tm") // 2)
    assert heights == 2
    _, frames, rows, channels, cols = clip_input.shape
    taps = first_kernel.shape[0]

    def forward(kernel):
        split = kernel.reshape(3, 9 * channels, channels)
        return jnp.swapaxes(split, 1, 2)

    def backward(kernel):
        split = kernel.reshape(3, 3, 3, channels, channels)[::-1, ::-1, ::-1]
        return jnp.transpose(split, (0, 3, 1, 2, 4)).reshape(3, channels, 9 * channels)

    chunk = taps // dp
    block = -(-chunk // (heights * depth * 16)) * 16
    padded = heights * depth * block
    copies = 1 + (dp - 1) + 2 + 2 * (depth - 1) + 1
    tile = (channels, cols)
    field = pltpu.VMEM((frames + 2, rows + 2, 3 * channels, cols), jnp.bfloat16)
    own = (frames, rows) + tile
    vmem = pl.BlockSpec(memory_space=pltpu.VMEM)
    block_output, input_grad, total = pl.pallas_call(
        functools.partial(body, (dp, heights, depth)),
        out_shape=(
            jax.ShapeDtypeStruct(own, jnp.float32),
            jax.ShapeDtypeStruct(own, jnp.float32),
            jax.ShapeDtypeStruct((2, heights, depth, block, channels), jnp.float32),
        ),
        in_specs=[vmem] * 6,
        out_specs=(vmem, vmem, vmem),
        scratch_shapes=[
            field,
            field,
            field,
            field,
            pltpu.VMEM(own, jnp.float32),
            pltpu.VMEM(own, jnp.bfloat16),
            pltpu.VMEM(own, jnp.bfloat16),
            pltpu.VMEM((4, 2, rows) + tile, jnp.bfloat16),
            pltpu.VMEM((4, frames) + tile, jnp.bfloat16),
            pltpu.VMEM((4, 2) + tile, jnp.bfloat16),
            pltpu.VMEM((2, taps, channels), jnp.float32),
            pltpu.VMEM((taps, channels), jnp.float32),
            pltpu.VMEM((dp, padded, channels), jnp.float32),
            pltpu.VMEM((dp, padded, channels), jnp.bfloat16),
            pltpu.VMEM((dp - 1, padded, channels), jnp.bfloat16),
            pltpu.VMEM((heights, depth * block, channels), jnp.bfloat16),
            pltpu.VMEM((depth * block, channels), jnp.bfloat16),
            pltpu.VMEM((depth, block, channels), jnp.float32),
            pltpu.VMEM((depth - 1, block, channels), jnp.float32),
            pltpu.VMEM((2, heights, depth, block, channels), jnp.bfloat16),
            pltpu.SemaphoreType.DMA((4, 3)),
            pltpu.SemaphoreType.DMA((4, 3)),
            pltpu.SemaphoreType.DMA((copies,)),
            pltpu.SemaphoreType.DMA((copies,)),
        ],
        compiler_params=pltpu.CompilerParams(collective_id=0, has_side_effects=True),
        name="block_step",
    )(
        clip_input[0],
        cotangent[0],
        forward(first_kernel),
        forward(second_kernel),
        backward(first_kernel),
        backward(second_kernel),
    )
    positions = frames * rows * cols * dp * heights * lax.axis_size("tm")
    factor = 1.0 / math.sqrt(positions)
    flat = total.reshape(2, padded, channels)[:, :chunk] * factor
    return (block_output[None], input_grad[None], flat[0], flat[1])


def solution(mesh):
    split = P("dp", "tm", "height", None, None)
    return jax.shard_map(
        local,
        mesh=mesh,
        in_specs=(split, split, P(), P()),
        out_specs=(split, split, P("dp", None), P("dp", None)),
        check_vma=False,
    )
```

```python
import functools
import math

import jax
import jax.numpy as jnp
from jax import lax
from jax.experimental import pallas as pl
from jax.experimental.pallas import tpu as pltpu
from jax.sharding import PartitionSpec as P

EPSILON = 1e-06
MESH_IDS = pl.DeviceIdType.MESH


def factor_of(value):
    return lax.rsqrt(jnp.mean(value * value, axis=0, keepdims=True) + EPSILON)


def act(value):
    scaled = value * factor_of(value)
    return scaled / (1.0 + jnp.exp(-scaled))


def act_back(value, grad):
    factor = factor_of(value)
    scaled = value * factor
    gate = 1.0 / (1.0 + jnp.exp(-scaled))
    inner = grad * (gate * (1.0 + scaled * (1.0 - gate)))
    return factor * (inner - scaled * jnp.mean(inner * scaled, axis=0, keepdims=True))


def body(
    sizes,
    x,
    cot,
    kernel_one,
    kernel_two,
    plain_one,
    plain_two,
    block_out,
    input_out,
    total,
    flip_one,
    flip_two,
    acts_one,
    acts_two,
    grads_two,
    grads_one,
    middle,
    second_act,
    middle_grad,
    time_halo,
    row_halo,
    corner_halo,
    terms,
    first,
    wide,
    narrow_dp,
    got_dp,
    narrow_h,
    got_h,
    wide_z,
    narrow_z,
    got_z,
    mine,
    halo_send,
    halo_recv,
    send,
    recv,
):
    dp, heights, depth = sizes
    frames, rows, channels, cols = x.shape
    shards = 2 * depth
    chunk = terms.shape[1] // dp
    shard = lax.axis_index("tm")
    core, level = shard % 2, shard // 2
    clip, half = lax.axis_index("dp"), lax.axis_index("height")
    other = 1 - half
    has_before, has_after = shard > 0, shard < shards - 1
    edge_row = (rows - 1) * other
    halo_row = (rows + 1) * other
    rim_row = (rows + 1) * half

    barrier = pltpu.get_barrier_semaphore()
    partner = {"tm": level * 2 + 1 - core}
    clip_peers = [(clip + step) % dp for step in range(1, dp)]
    level_peers = [(level + step) % depth for step in range(1, depth)]
    places = [partner, {"height": other}]
    places += [{"dp": peer} for peer in clip_peers]
    places += [{"tm": peer * 2 + core} for peer in level_peers]

    def greet(place):
        pl.semaphore_signal(barrier, inc=1, device_id=place, device_id_type=MESH_IDS)

    for place in places:
        greet(place)

    outer = shard + 2 * core - 1
    has_outer = jnp.logical_and(outer >= 0, outer < shards)

    @pl.when(has_outer)
    def _():
        greet({"tm": outer})

    @pl.when(has_before)
    def _():
        greet({"tm": shard - 1, "height": other})

    @pl.when(has_after)
    def _():
        greet({"tm": shard + 1, "height": other})

    near = has_outer.astype(jnp.int32) + has_before.astype(jnp.int32) + has_after.astype(jnp.int32)
    pl.semaphore_wait(barrier, len(places) + near)

    def remote(source, target, sender, receiver, place):
        return pltpu.make_async_remote_copy(
            src_ref=source,
            dst_ref=target,
            send_sem=sender,
            recv_sem=receiver,
            device_id=place,
            device_id_type=MESH_IDS,
        )

    def exchange(own, slot, ahead):
        step = -1 if ahead else 1
        start = 0 if ahead else frames - 2
        goes, comes = (has_before, has_after) if ahead else (has_after, has_before)
        span = pl.ds(start, 2)
        along = remote(own.at[span], time_halo.at[slot], halo_send.at[slot, 0], halo_recv.at[slot, 0], {"tm": shard + step})
        across = remote(own.at[:, edge_row], row_halo.at[slot], halo_send.at[slot, 1], halo_recv.at[slot, 1], {"height": other})
        corner = remote(
            own.at[span, edge_row],
            corner_halo.at[slot],
            halo_send.at[slot, 2],
            halo_recv.at[slot, 2],
            {"tm": shard + step, "height": other},
        )
        across.start()

        @pl.when(goes)
        def _():
            along.start()
            corner.start()

        def arrive():
            across.wait()

            @pl.when(goes)
            def _():
                along.wait_send()
                corner.wait_send()

            @pl.when(comes)
            def _():
                along.wait_recv()
                corner.wait_recv()

        return arrive

    lane = lax.broadcasted_iota(jnp.int32, (channels, cols), 1)

    def place_tile(field, frame, row, value):
        wide_value = value.astype(jnp.float32)
        left = jnp.where(lane == 0, 0.0, pltpu.roll(wide_value, 1, axis=1))
        right = jnp.where(lane == cols - 1, 0.0, pltpu.roll(wide_value, cols - 1, axis=1))
        field[frame, row, 0:channels] = left.astype(jnp.bfloat16)
        field[frame, row, channels : 2 * channels] = value
        field[frame, row, 2 * channels : 3 * channels] = right.astype(jnp.bfloat16)

    def fill_halo(field, slot, ahead, make):
        inside, outside = (0, frames) if ahead else (2, 0)
        comes = has_after if ahead else has_before
        blank = jnp.zeros((3 * channels, cols), jnp.bfloat16)
        for frame in range(frames + 2):
            field[frame, rim_row] = blank

        def row_step(frame, carry):
            place_tile(field, inside + frame, halo_row, make(row_halo[slot, frame]))
            return carry

        lax.fori_loop(0, frames, row_step, 0)

        @pl.when(comes)
        def _():
            def time_step(index, carry):
                frame, row = index // rows, index % rows
                place_tile(field, outside + frame, row + 1, make(time_halo[slot, frame, row]))
                return carry

            lax.fori_loop(0, 2 * rows, time_step, 0)
            for frame in range(2):
                place_tile(field, outside + frame, halo_row, make(corner_halo[slot, frame]))

        @pl.when(jnp.logical_not(comes))
        def _():
            for frame in range(2):
                for row in range(rows + 2):
                    field[outside + frame, row] = blank

    def conv(field, kernel, finish):
        def step(index, carry):
            frame, row = 2 * (index // rows), index % rows
            summed = None
            for tap in range(3):
                pair = [
                    field[frame + tap + side, pl.ds(row, 3)].reshape(9 * channels, cols) for side in range(2)
                ]
                part = jnp.dot(kernel[tap], jnp.concatenate(pair, axis=1), preferred_element_type=jnp.float32)
                summed = part if summed is None else summed + part
            for side in range(2):
                finish(frame + side, row, summed[:, side * cols : (side + 1) * cols])
            return carry

        lax.fori_loop(0, frames // 2 * rows, step, 0)

    def kernel_grad(slot, field, grad):
        def step(index, carry):
            tap, tap_row = index // 3, index % 3
            tiles = [(frame, row) for frame in range(frames) for row in range(rows)]
            left = jnp.concatenate([field[frame + tap, row + tap_row] for frame, row in tiles], axis=1)
            right = jnp.concatenate([grad[frame, row] for frame, row in tiles], axis=1)
            piece = lax.dot_general(left, right, (((1,), (1,)), ((), ())), preferred_element_type=jnp.float32)
            terms[slot, pl.ds(pl.multiple_of(index * 3 * channels, 3 * channels), 3 * channels)] = piece
            return carry

        lax.fori_loop(0, 9, step, 0)

    def as_act(value):
        return act(value.astype(jnp.float32)).astype(jnp.bfloat16)

    x_arrives = exchange(x, 0, False)
    cot_arrives = exchange(cot, 1, True)

    def first_step(index, carry):
        frame, row = index // rows, index % rows
        place_tile(acts_one, frame + 2, row + 1, as_act(x[frame, row]))
        place_tile(grads_two, frame, row + 1, cot[frame, row])
        return carry

    lax.fori_loop(0, frames * rows, first_step, 0)
    for plain, flip in ((plain_two, flip_two), (plain_one, flip_one)):
        for index in range(27):
            tile = plain[(26 - index) * channels : (27 - index) * channels]
            flip[index // 9, :, (index % 9) * channels : (index % 9 + 1) * channels] = tile
    x_arrives()
    fill_halo(acts_one, 0, False, as_act)

    def finish_middle(frame, row, value):
        middle[frame, row] = value
        rounded = act(value).astype(jnp.bfloat16)
        second_act[frame, row] = rounded
        place_tile(acts_two, frame + 2, row + 1, rounded)

    conv(acts_one, kernel_one, finish_middle)
    act_arrives = exchange(second_act, 2, False)
    cot_arrives()
    fill_halo(grads_two, 1, True, lambda value: value)

    def finish_back(frame, row, value):
        rounded = act_back(middle[frame, row], value).astype(jnp.bfloat16)
        middle_grad[frame, row] = rounded
        place_tile(grads_one, frame, row + 1, rounded)

    conv(grads_two, flip_two, finish_back)
    grad_arrives = exchange(middle_grad, 3, True)

    used = [0]

    def send_to(source, target, place):
        slot = used[0]
        used[0] += 1
        copy = remote(source, target, send.at[slot], recv.at[slot], place)
        copy.start()
        return copy

    kernel_grad(0, acts_one, middle_grad)
    act_arrives()
    fill_halo(acts_two, 2, False, lambda value: value)
    kernel_grad(1, acts_two, cot)
    swap = send_to(terms.at[1 - core], first, partner)

    def finish_branch(frame, row, value):
        block_out[frame, row] = x[frame, row].astype(jnp.float32) + value

    def finish_input(frame, row, value):
        back = act_back(x[frame, row].astype(jnp.float32), value)
        input_out[frame, row] = cot[frame, row].astype(jnp.float32) + back

    conv(acts_two, kernel_two, finish_branch)
    swap.wait()
    padded = wide.shape[1]
    for index in range(dp):
        span = pl.ds(index * chunk, chunk)
        summed = terms[core, span] + first[span]
        if padded > chunk:
            summed = jnp.concatenate([summed, jnp.zeros((padded - chunk, channels), jnp.float32)], axis=0)
        wide[index] = summed
        narrow_dp[index] = summed.astype(jnp.bfloat16)
    copies = [send_to(narrow_dp.at[peer], got_dp.at[i], {"dp": peer}) for i, peer in enumerate(clip_peers)]
    grad_arrives()
    fill_halo(grads_one, 3, True, lambda value: value)
    conv(grads_one, flip_one, finish_input)
    for copy in copies:
        copy.wait()
    summed = wide[clip]
    for i in range(dp - 1):
        summed = summed + got_dp[i].astype(jnp.float32)
    wide[0] = summed
    narrow_h[...] = summed.astype(jnp.bfloat16).reshape(narrow_h.shape)
    send_to(narrow_h.at[other], got_h, {"height": other}).wait()
    block = wide_z.shape[1]
    mine_rows = pl.ds(pl.multiple_of(half * (depth * block), depth * block), depth * block)
    summed = wide[0, mine_rows] + got_h[...].astype(jnp.float32)
    wide_z[...] = summed.reshape(wide_z.shape)
    narrow_z[...] = summed.reshape(wide_z.shape).astype(jnp.bfloat16)
    copies = [
        send_to(narrow_z.at[peer], got_z.at[i], {"tm": peer * 2 + core}) for i, peer in enumerate(level_peers)
    ]
    for copy in copies:
        copy.wait()
    summed = wide_z[level]
    for i in range(depth - 1):
        summed = summed + got_z[i].astype(jnp.float32)
    mine[core, half, level] = summed.astype(jnp.bfloat16)
    own = mine.at[core, half, level]
    copies = [send_to(own, own, {"tm": peer * 2 + core}) for peer in level_peers]
    for copy in copies:
        copy.wait()
    own = mine.at[core, half]
    send_to(own, own, {"height": other}).wait()
    own = mine.at[core]
    send_to(own, own, partner).wait()
    total[...] = mine[...].astype(jnp.float32)


def local(clip_input, cotangent, first_kernel, second_kernel):
    dp, heights, depth = (lax.axis_size("dp"), lax.axis_size("height"), lax.axis_size("tm") // 2)
    assert heights == 2
    _, frames, rows, channels, cols = clip_input.shape
    taps = first_kernel.shape[0]

    def forward(kernel):
        split = kernel.reshape(3, 9 * channels, channels)
        return jnp.swapaxes(split, 1, 2)

    chunk = taps // dp
    block = -(-chunk // (heights * depth * 16)) * 16
    padded = heights * depth * block
    copies = 1 + (dp - 1) + 2 + 2 * (depth - 1) + 1
    tile = (channels, cols)
    field = pltpu.VMEM((frames + 2, rows + 2, 3 * channels, cols), jnp.bfloat16)
    own = (frames, rows) + tile
    vmem = pl.BlockSpec(memory_space=pltpu.VMEM)
    block_output, input_grad, total = pl.pallas_call(
        functools.partial(body, (dp, heights, depth)),
        out_shape=(
            jax.ShapeDtypeStruct(own, jnp.float32),
            jax.ShapeDtypeStruct(own, jnp.float32),
            jax.ShapeDtypeStruct((2, heights, depth, block, channels), jnp.float32),
        ),
        in_specs=[vmem] * 6,
        out_specs=(vmem, vmem, vmem),
        scratch_shapes=[
            pltpu.VMEM((3, channels, 9 * channels), jnp.bfloat16),
            pltpu.VMEM((3, channels, 9 * channels), jnp.bfloat16),
            field,
            field,
            field,
            field,
            pltpu.VMEM(own, jnp.float32),
            pltpu.VMEM(own, jnp.bfloat16),
            pltpu.VMEM(own, jnp.bfloat16),
            pltpu.VMEM((4, 2, rows) + tile, jnp.bfloat16),
            pltpu.VMEM((4, frames) + tile, jnp.bfloat16),
            pltpu.VMEM((4, 2) + tile, jnp.bfloat16),
            pltpu.VMEM((2, taps, channels), jnp.float32),
            pltpu.VMEM((taps, channels), jnp.float32),
            pltpu.VMEM((dp, padded, channels), jnp.float32),
            pltpu.VMEM((dp, padded, channels), jnp.bfloat16),
            pltpu.VMEM((dp - 1, padded, channels), jnp.bfloat16),
            pltpu.VMEM((heights, depth * block, channels), jnp.bfloat16),
            pltpu.VMEM((depth * block, channels), jnp.bfloat16),
            pltpu.VMEM((depth, block, channels), jnp.float32),
            pltpu.VMEM((depth, block, channels), jnp.bfloat16),
            pltpu.VMEM((depth - 1, block, channels), jnp.bfloat16),
            pltpu.VMEM((2, heights, depth, block, channels), jnp.bfloat16),
            pltpu.SemaphoreType.DMA((4, 3)),
            pltpu.SemaphoreType.DMA((4, 3)),
            pltpu.SemaphoreType.DMA((copies,)),
            pltpu.SemaphoreType.DMA((copies,)),
        ],
        compiler_params=pltpu.CompilerParams(collective_id=0, has_side_effects=True),
        name="block_step",
    )(
        clip_input[0],
        cotangent[0],
        forward(first_kernel),
        forward(second_kernel),
        first_kernel,
        second_kernel,
    )
    positions = frames * rows * cols * dp * heights * lax.axis_size("tm")
    factor = 1.0 / math.sqrt(positions)
    flat = total.reshape(2, padded, channels)[:, :chunk] * factor
    return (block_output[None], input_grad[None], flat[0], flat[1])


def solution(mesh):
    split = P("dp", "tm", "height", None, None)
    return jax.shard_map(
        local,
        mesh=mesh,
        in_specs=(split, split, P(), P()),
        out_specs=(split, split, P("dp", None), P("dp", None)),
        check_vma=False,
    )
```

```python
import functools
import math

import jax
import jax.numpy as jnp
from jax import lax
from jax.experimental import pallas as pl
from jax.experimental.pallas import tpu as pltpu
from jax.sharding import PartitionSpec as P

EPSILON = 1e-06
MESH_IDS = pl.DeviceIdType.MESH


def factor_of(value):
    return lax.rsqrt(jnp.mean(value * value, axis=0, keepdims=True) + EPSILON)


def act(value):
    scaled = value * factor_of(value)
    return scaled / (1.0 + jnp.exp(-scaled))


def act_back(value, grad):
    factor = factor_of(value)
    scaled = value * factor
    gate = 1.0 / (1.0 + jnp.exp(-scaled))
    inner = grad * (gate * (1.0 + scaled * (1.0 - gate)))
    return factor * (inner - scaled * jnp.mean(inner * scaled, axis=0, keepdims=True))


def body(
    sizes,
    x,
    cot,
    kernel_one,
    kernel_two,
    plain_one,
    plain_two,
    block_out,
    input_out,
    total,
    flip_one,
    flip_two,
    acts_one,
    acts_two,
    grads_two,
    grads_one,
    middle,
    second_act,
    middle_grad,
    time_halo,
    row_halo,
    corner_halo,
    terms,
    first,
    wide,
    narrow_dp,
    got_dp,
    narrow_h,
    got_h,
    wide_z,
    narrow_z,
    got_z,
    mine,
    halo_send,
    halo_recv,
    send,
    recv,
):
    dp, heights, depth = sizes
    frames, rows, channels, cols = x.shape
    shards = 2 * depth
    chunk = terms.shape[1] // dp
    shard = lax.axis_index("tm")
    core, level = shard % 2, shard // 2
    clip, half = lax.axis_index("dp"), lax.axis_index("height")
    other = 1 - half
    has_before, has_after = shard > 0, shard < shards - 1
    edge_row = (rows - 1) * other
    halo_row = (rows + 1) * other
    rim_row = (rows + 1) * half

    barrier = pltpu.get_barrier_semaphore()
    partner = {"tm": level * 2 + 1 - core}
    clip_peers = [(clip + step) % dp for step in range(1, dp)]
    level_peers = [(level + step) % depth for step in range(1, depth)]
    places = [partner, {"height": other}]
    places += [{"dp": peer} for peer in clip_peers]
    places += [{"tm": peer * 2 + core} for peer in level_peers]

    def greet(place):
        pl.semaphore_signal(barrier, inc=1, device_id=place, device_id_type=MESH_IDS)

    for place in places:
        greet(place)

    outer = shard + 2 * core - 1
    has_outer = jnp.logical_and(outer >= 0, outer < shards)

    @pl.when(has_outer)
    def _():
        greet({"tm": outer})

    @pl.when(has_before)
    def _():
        greet({"tm": shard - 1, "height": other})

    @pl.when(has_after)
    def _():
        greet({"tm": shard + 1, "height": other})

    near = has_outer.astype(jnp.int32) + has_before.astype(jnp.int32) + has_after.astype(jnp.int32)
    pl.semaphore_wait(barrier, len(places) + near)

    def remote(source, target, sender, receiver, place):
        return pltpu.make_async_remote_copy(
            src_ref=source,
            dst_ref=target,
            send_sem=sender,
            recv_sem=receiver,
            device_id=place,
            device_id_type=MESH_IDS,
        )

    def exchange(own, slot, ahead):
        step = -1 if ahead else 1
        start = 0 if ahead else frames - 2
        goes, comes = (has_before, has_after) if ahead else (has_after, has_before)
        span = pl.ds(start, 2)
        along = remote(own.at[span], time_halo.at[slot], halo_send.at[slot, 0], halo_recv.at[slot, 0], {"tm": shard + step})
        across = remote(own.at[:, edge_row], row_halo.at[slot], halo_send.at[slot, 1], halo_recv.at[slot, 1], {"height": other})
        corner = remote(
            own.at[span, edge_row],
            corner_halo.at[slot],
            halo_send.at[slot, 2],
            halo_recv.at[slot, 2],
            {"tm": shard + step, "height": other},
        )
        across.start()

        @pl.when(goes)
        def _():
            along.start()
            corner.start()

        def arrive():
            across.wait()

            @pl.when(goes)
            def _():
                along.wait_send()
                corner.wait_send()

            @pl.when(comes)
            def _():
                along.wait_recv()
                corner.wait_recv()

        return arrive

    lane = lax.broadcasted_iota(jnp.int32, (channels, cols), 1)

    def place_tile(field, frame, row, value):
        wide_value = value.astype(jnp.float32)
        left = jnp.where(lane == 0, 0.0, pltpu.roll(wide_value, 1, axis=1))
        right = jnp.where(lane == cols - 1, 0.0, pltpu.roll(wide_value, cols - 1, axis=1))
        field[frame, row, 0:channels] = left.astype(jnp.bfloat16)
        field[frame, row, channels : 2 * channels] = value
        field[frame, row, 2 * channels : 3 * channels] = right.astype(jnp.bfloat16)

    def fill_halo(field, slot, ahead, make):
        inside, outside = (0, frames) if ahead else (2, 0)
        comes = has_after if ahead else has_before
        blank = jnp.zeros((3 * channels, cols), jnp.bfloat16)
        for frame in range(frames + 2):
            field[frame, rim_row] = blank

        def row_step(frame, carry):
            place_tile(field, inside + frame, halo_row, make(row_halo[slot, frame]))
            return carry

        lax.fori_loop(0, frames, row_step, 0)

        @pl.when(comes)
        def _():
            def time_step(index, carry):
                frame, row = index // rows, index % rows
                place_tile(field, outside + frame, row + 1, make(time_halo[slot, frame, row]))
                return carry

            lax.fori_loop(0, 2 * rows, time_step, 0)
            for frame in range(2):
                place_tile(field, outside + frame, halo_row, make(corner_halo[slot, frame]))

        @pl.when(jnp.logical_not(comes))
        def _():
            for frame in range(2):
                for row in range(rows + 2):
                    field[outside + frame, row] = blank

    steps = frames // 2 * rows

    def conv(field, kernel, finish, begin=0, end=steps):
        def step(index, carry):
            frame, row = 2 * (index // rows), index % rows
            summed = None
            for tap in range(3):
                pair = [
                    field[frame + tap + side, pl.ds(row, 3)].reshape(9 * channels, cols) for side in range(2)
                ]
                part = jnp.dot(kernel[tap], jnp.concatenate(pair, axis=1), preferred_element_type=jnp.float32)
                summed = part if summed is None else summed + part
            for side in range(2):
                finish(frame + side, row, summed[:, side * cols : (side + 1) * cols])
            return carry

        lax.fori_loop(begin, end, step, 0)

    def kernel_grad(slot, field, grad):
        def step(index, carry):
            tap, tap_row = index // 3, index % 3
            tiles = [(frame, row) for frame in range(frames) for row in range(rows)]
            left = jnp.concatenate([field[frame + tap, row + tap_row] for frame, row in tiles], axis=1)
            right = jnp.concatenate([grad[frame, row] for frame, row in tiles], axis=1)
            piece = lax.dot_general(left, right, (((1,), (1,)), ((), ())), preferred_element_type=jnp.float32)
            terms[slot, pl.ds(pl.multiple_of(index * 3 * channels, 3 * channels), 3 * channels)] = piece
            return carry

        lax.fori_loop(0, 9, step, 0)

    def as_act(value):
        return act(value.astype(jnp.float32)).astype(jnp.bfloat16)

    x_arrives = exchange(x, 0, False)
    cot_arrives = exchange(cot, 1, True)

    def first_step(index, carry):
        frame, row = index // rows, index % rows
        place_tile(acts_one, frame + 2, row + 1, as_act(x[frame, row]))
        place_tile(grads_two, frame, row + 1, cot[frame, row])
        return carry

    lax.fori_loop(0, frames * rows, first_step, 0)
    for plain, flip in ((plain_two, flip_two), (plain_one, flip_one)):
        for index in range(27):
            tile = plain[(26 - index) * channels : (27 - index) * channels]
            flip[index // 9, :, (index % 9) * channels : (index % 9 + 1) * channels] = tile
    x_arrives()
    fill_halo(acts_one, 0, False, as_act)

    def finish_middle(frame, row, value):
        middle[frame, row] = value
        rounded = act(value).astype(jnp.bfloat16)
        second_act[frame, row] = rounded
        place_tile(acts_two, frame + 2, row + 1, rounded)

    conv(acts_one, kernel_one, finish_middle)
    act_arrives = exchange(second_act, 2, False)
    cot_arrives()
    fill_halo(grads_two, 1, True, lambda value: value)

    def finish_back(frame, row, value):
        rounded = act_back(middle[frame, row], value).astype(jnp.bfloat16)
        middle_grad[frame, row] = rounded
        place_tile(grads_one, frame, row + 1, rounded)

    conv(grads_two, flip_two, finish_back)
    grad_arrives = exchange(middle_grad, 3, True)

    used = [0]

    def send_to(source, target, place):
        slot = used[0]
        used[0] += 1
        copy = remote(source, target, send.at[slot], recv.at[slot], place)
        copy.start()
        return copy

    kernel_grad(0, acts_one, middle_grad)
    act_arrives()
    fill_halo(acts_two, 2, False, lambda value: value)
    kernel_grad(1, acts_two, cot)
    swap = send_to(terms.at[1 - core], first, partner)

    def finish_branch(frame, row, value):
        block_out[frame, row] = x[frame, row].astype(jnp.float32) + value

    def finish_input(frame, row, value):
        back = act_back(x[frame, row].astype(jnp.float32), value)
        input_out[frame, row] = cot[frame, row].astype(jnp.float32) + back

    conv(acts_two, kernel_two, finish_branch, 0, steps // 2)
    swap.wait()
    padded = wide.shape[1]
    for index in range(dp):
        span = pl.ds(index * chunk, chunk)
        summed = terms[core, span] + first[span]
        if padded > chunk:
            summed = jnp.concatenate([summed, jnp.zeros((padded - chunk, channels), jnp.float32)], axis=0)
        wide[index] = summed
        narrow_dp[index] = summed.astype(jnp.bfloat16)
    copies = [send_to(narrow_dp.at[peer], got_dp.at[i], {"dp": peer}) for i, peer in enumerate(clip_peers)]
    conv(acts_two, kernel_two, finish_branch, steps // 2, steps)
    grad_arrives()
    fill_halo(grads_one, 3, True, lambda value: value)
    conv(grads_one, flip_one, finish_input, 0, steps // 2)
    for copy in copies:
        copy.wait()
    summed = wide[clip]
    for i in range(dp - 1):
        summed = summed + got_dp[i].astype(jnp.float32)
    wide[0] = summed
    narrow_h[...] = summed.astype(jnp.bfloat16).reshape(narrow_h.shape)
    copy = send_to(narrow_h.at[other], got_h, {"height": other})
    conv(grads_one, flip_one, finish_input, steps // 2, steps)
    copy.wait()
    block = wide_z.shape[1]
    mine_rows = pl.ds(pl.multiple_of(half * (depth * block), depth * block), depth * block)
    summed = wide[0, mine_rows] + got_h[...].astype(jnp.float32)
    wide_z[...] = summed.reshape(wide_z.shape)
    narrow_z[...] = summed.reshape(wide_z.shape).astype(jnp.bfloat16)
    copies = [
        send_to(narrow_z.at[peer], got_z.at[i], {"tm": peer * 2 + core}) for i, peer in enumerate(level_peers)
    ]
    for copy in copies:
        copy.wait()
    summed = wide_z[level]
    for i in range(depth - 1):
        summed = summed + got_z[i].astype(jnp.float32)
    mine[core, half, level] = summed.astype(jnp.bfloat16)
    own = mine.at[core, half, level]
    copies = [send_to(own, own, {"tm": peer * 2 + core}) for peer in level_peers]
    for copy in copies:
        copy.wait()
    own = mine.at[core, half]
    send_to(own, own, {"height": other}).wait()
    own = mine.at[core]
    send_to(own, own, partner).wait()
    total[...] = mine[...].astype(jnp.float32)


def local(clip_input, cotangent, first_kernel, second_kernel):
    dp, heights, depth = (lax.axis_size("dp"), lax.axis_size("height"), lax.axis_size("tm") // 2)
    assert heights == 2
    _, frames, rows, channels, cols = clip_input.shape
    taps = first_kernel.shape[0]

    def forward(kernel):
        split = kernel.reshape(3, 9 * channels, channels)
        return jnp.swapaxes(split, 1, 2)

    chunk = taps // dp
    block = -(-chunk // (heights * depth * 16)) * 16
    padded = heights * depth * block
    copies = 1 + (dp - 1) + 2 + 2 * (depth - 1) + 1
    tile = (channels, cols)
    field = pltpu.VMEM((frames + 2, rows + 2, 3 * channels, cols), jnp.bfloat16)
    own = (frames, rows) + tile
    vmem = pl.BlockSpec(memory_space=pltpu.VMEM)
    block_output, input_grad, total = pl.pallas_call(
        functools.partial(body, (dp, heights, depth)),
        out_shape=(
            jax.ShapeDtypeStruct(own, jnp.float32),
            jax.ShapeDtypeStruct(own, jnp.float32),
            jax.ShapeDtypeStruct((2, heights, depth, block, channels), jnp.float32),
        ),
        in_specs=[vmem] * 6,
        out_specs=(vmem, vmem, vmem),
        scratch_shapes=[
            pltpu.VMEM((3, channels, 9 * channels), jnp.bfloat16),
            pltpu.VMEM((3, channels, 9 * channels), jnp.bfloat16),
            field,
            field,
            field,
            field,
            pltpu.VMEM(own, jnp.float32),
            pltpu.VMEM(own, jnp.bfloat16),
            pltpu.VMEM(own, jnp.bfloat16),
            pltpu.VMEM((4, 2, rows) + tile, jnp.bfloat16),
            pltpu.VMEM((4, frames) + tile, jnp.bfloat16),
            pltpu.VMEM((4, 2) + tile, jnp.bfloat16),
            pltpu.VMEM((2, taps, channels), jnp.float32),
            pltpu.VMEM((taps, channels), jnp.float32),
            pltpu.VMEM((dp, padded, channels), jnp.float32),
            pltpu.VMEM((dp, padded, channels), jnp.bfloat16),
            pltpu.VMEM((dp - 1, padded, channels), jnp.bfloat16),
            pltpu.VMEM((heights, depth * block, channels), jnp.bfloat16),
            pltpu.VMEM((depth * block, channels), jnp.bfloat16),
            pltpu.VMEM((depth, block, channels), jnp.float32),
            pltpu.VMEM((depth, block, channels), jnp.bfloat16),
            pltpu.VMEM((depth - 1, block, channels), jnp.bfloat16),
            pltpu.VMEM((2, heights, depth, block, channels), jnp.bfloat16),
            pltpu.SemaphoreType.DMA((4, 3)),
            pltpu.SemaphoreType.DMA((4, 3)),
            pltpu.SemaphoreType.DMA((copies,)),
            pltpu.SemaphoreType.DMA((copies,)),
        ],
        compiler_params=pltpu.CompilerParams(collective_id=0, has_side_effects=True),
        name="block_step",
    )(
        clip_input[0],
        cotangent[0],
        forward(first_kernel),
        forward(second_kernel),
        first_kernel,
        second_kernel,
    )
    positions = frames * rows * cols * dp * heights * lax.axis_size("tm")
    factor = 1.0 / math.sqrt(positions)
    flat = total.reshape(2, padded, channels)[:, :chunk] * factor
    return (block_output[None], input_grad[None], flat[0], flat[1])


def solution(mesh):
    split = P("dp", "tm", "height", None, None)
    return jax.shard_map(
        local,
        mesh=mesh,
        in_specs=(split, split, P(), P()),
        out_specs=(split, split, P("dp", None), P("dp", None)),
        check_vma=False,
    )
```
